32 devices in a mesh: expert: 4 (over y, core), fsdp: 8 (over z, x).
Axes of the slice: x: 2, y: 2, z: 4, core: 2. Of those that a mesh axis runs over, the one named last changes fastest.
Arguments:
- layer_input: bfloat16 [8192, 2048], P(('expert', 'fsdp')), may hold values from -6 to 6
- expert_ids: int32 [8192, 8], P(('expert', 'fsdp')), may hold values from 0 to 15, as said below
- slot_ids: int32 [8192, 8], P(('expert', 'fsdp')), may hold values from 0 to 255, as said below
- attn_gain: float32 [2048], replicated, may hold values from 0.25 to 1.75
- qkv_weight: bfloat16 [2048, 6144], P('fsdp'), may hold values from -0.125 to 0.125
- query_gain: float32 [128], replicated, may hold values from 0.25 to 1.75
- key_gain: float32 [128], replicated, may hold values from 0.25 to 1.75
- out_weight: bfloat16 [2048, 2048], P('fsdp'), may hold values from -1 to 1
- ffn_gain: float32 [2048], replicated, may hold values from 0.25 to 1.75
- router_weight: bfloat16 [2048, 16], P('fsdp'), may hold values from -0.0625 to 0.0625
- gate_up_weight: bfloat16 [16, 2048, 2048], P('expert', 'fsdp'), may hold values from -0.125 to 0.125
- down_weight: bfloat16 [16, 1024, 2048], P('expert', 'fsdp'), may hold values from -0.75 to 0.75
- cotangent: bfloat16 [8192, 2048], P(('expert', 'fsdp')), may hold values from -6 to 6
Outputs:
- mixed_out: bfloat16 [8192, 2048], P(('expert', 'fsdp'))
- input_grad: float32 [8192, 2048], P(('expert', 'fsdp'))
- attn_gain_grad: float32 [2048], replicated
- qkv_weight_grad: float32 [2048, 6144], P('fsdp')
- query_gain_grad: float32 [128], replicated
- key_gain_grad: float32 [128], replicated
- out_weight_grad: float32 [2048, 2048], P('fsdp')
- ffn_gain_grad: float32 [2048], replicated
- router_weight_grad: float32 [2048, 16], P('fsdp')
- gate_up_grad: float32 [16, 2048, 2048], P('expert', 'fsdp')
- down_grad: float32 [16, 1024, 2048], P('expert', 'fsdp')
The draws below stay inside these ranges and needn't reach their ends.
Inputs may be any that keep to these rules, and one draw needn't show every extreme that they name: `expert_ids`: each row names 8 different experts. Among the 256 rows of one device no expert is named more than 256 times; in every device's rows one expert is named exactly 256 times. `slot_ids`: among the rows of one device, the routes to one expert have different slots.
All inputs are finite; a program needn't handle non-finite values.
Results may differ from the reference program's by a relative error of at most 0.022.
Values may be sent and summed in bfloat16 or wider, within the bound.
No kernel may reach another device: no remote copies, remote signals or barrier semaphores. Data moves between devices by JAX's collectives and lax.ppermute only.
A program may use at most 384 MiB of HBM per device.

```python
import jax
import jax.numpy as jnp
from jax import lax

D = 2048
H = 16
HD = 128
FF = 1024
TOPK = 8
TOK_DEV = 256
EXPERTS = 16
CAP = 256
TOKENS = 8192


def layout(key):
    blocks = TOKENS // TOK_DEV
    mean_load = TOK_DEV * TOPK // EXPERTS
    stride = 2 * mean_load // EXPERTS
    half_count = EXPERTS // 2
    rank_ids = jnp.arange(EXPERTS, dtype=jnp.int32)
    pair_index = jnp.minimum(rank_ids, EXPERTS - 1 - rank_ids)
    signed = jnp.where(rank_ids < half_count, 1, -1).astype(jnp.int32)
    base_load = mean_load + signed * stride * (half_count - pair_index)
    streams = jax.random.split(jax.random.fold_in(key, 7), 5)
    jitter = jax.random.randint(streams[0], (blocks, half_count), 0, max(stride, 1)).astype(jnp.int32)
    jitter = jitter.at[:, 0].set(0)
    load_counts = base_load[None, :] - signed[None, :] * jitter[:, pair_index]
    run_ends = jnp.cumsum(load_counts, 1)
    starts = run_ends - load_counts
    position = jnp.arange(TOK_DEV * TOPK, dtype=jnp.int32)
    run_index = jnp.sum((run_ends[:, None, :] <= position[None, :, None]).astype(jnp.int32), 2)
    offset = position[None, :] - jnp.take_along_axis(starts, run_index, 1)
    heavy_expert = jax.random.randint(streams[1], (), 0, EXPERTS).astype(jnp.int32)

    def relabel(stream):
        label_order = jax.random.permutation(stream, EXPERTS).astype(jnp.int32)
        heavy_spot = jnp.argmax(label_order == heavy_expert)
        return label_order.at[heavy_spot].set(label_order[0]).at[0].set(heavy_expert)
    labels = jax.vmap(relabel)(jax.random.split(streams[2], blocks))
    chosen = jnp.take_along_axis(labels, run_index, 1)
    chosen = chosen.reshape(blocks, TOPK, TOK_DEV).transpose(0, 2, 1)
    offset = offset.reshape(blocks, TOPK, TOK_DEV).transpose(0, 2, 1)
    scores = jax.random.randint(streams[3], (blocks, TOK_DEV, TOPK), 0, 4096).astype(jnp.int32) * TOPK + jnp.arange(TOPK, dtype=jnp.int32)
    column = jnp.argsort(scores, -1)
    chosen = jnp.take_along_axis(chosen, column, 2)
    offset = jnp.take_along_axis(offset, column, 2)

    def shuffle(stream):
        return jax.random.permutation(stream, TOK_DEV).astype(jnp.int32)
    row_order = jax.vmap(shuffle)(jax.random.split(streams[4], blocks))
    chosen = jnp.take_along_axis(chosen, row_order[:, :, None], 1)
    offset = jnp.take_along_axis(offset, row_order[:, :, None], 1)
    return (chosen.reshape(TOKENS, TOPK).astype(jnp.int32), offset.reshape(TOKENS, TOPK).astype(jnp.int32))


def draw_expert_ids(key, part):
    return layout(key)[0]


def draw_slot_ids(key, part):
    return layout(key)[1]


def spiked(entries, stream_key, source, target, shards_of, factor):
    owner, partner = [(jnp.arange(entries.shape[dim]) // (entries.shape[dim] // shards_of)).reshape([-1 if axis == dim else 1 for axis in range(entries.ndim)]) for dim in (source, target)]
    chosen = jax.random.permutation(stream_key, shards_of)[partner]
    strong = (owner == chosen) | (owner == (partner + shards_of // 2) % shards_of)
    return jnp.where(strong, factor * entries, entries)


def block_levels(rng, shape, shards, smallest, top_value):
    level, own = 1.0, jax.random.fold_in(rng, 6)
    for dim, parts in shards:
        heights = jnp.exp(jax.random.uniform(jax.random.fold_in(own, dim), (parts,), jnp.float32, smallest / len(shards), top_value / len(shards)))
        level = level * jnp.repeat(heights, shape[dim] // parts).reshape([-1 if axis == dim else 1 for axis in range(len(shape))])
    return level


def normal_values(own_key, shape, spread, reach, cuts=(), kind=jnp.bfloat16):
    result = jax.random.normal(own_key, shape, jnp.float32) * spread
    if len(cuts) > 0:
        result = block_levels(own_key, shape, cuts, -0.22, 0.18) * result
    return jnp.clip(result, min=-reach, max=reach).astype(kind)


def noise_with(stream_key, dims, scale, most, shards, heavy, kind=jnp.bfloat16):
    result = scale * jax.random.normal(stream_key, dims, jnp.float32)
    if shards:
        result = result * block_levels(stream_key, dims, shards, -0.22, 0.18)
    return jnp.clip(spiked(result, jax.random.fold_in(stream_key, 3), *heavy), -most, most).astype(kind)


def setup_inputs(seed: int = 0) -> dict:
    key_list = jax.random.split(jax.random.key(seed), 14)
    return {
        "layer_input": noise_with(key_list[0], (TOKENS, D), 1.0, 6.0, ((0, 32),), (0, 1, 32, 2.75)),
        "expert_ids": draw_expert_ids(jax.random.fold_in(key_list[13], 71), 0),
        "slot_ids": draw_slot_ids(jax.random.fold_in(key_list[13], 71), 0),
        "attn_gain": jnp.clip(1.0 + 0.15 * jax.random.normal(key_list[3], (D,), jnp.float32), 0.25, 1.75),
        "qkv_weight": normal_values(key_list[4], (D, 3 * D), D ** -0.5, 0.125, ((0, 8),)),
        "query_gain": jnp.clip(1.0 + 0.15 * jax.random.normal(key_list[5], (HD,), jnp.float32), 0.25, 1.75),
        "key_gain": jnp.clip(1.0 + 0.15 * jax.random.normal(key_list[6], (HD,), jnp.float32), 0.25, 1.75),
        "out_weight": normal_values(key_list[7], (D, D), (D * 4 // TOK_DEV) ** -0.5, 1.0, ((0, 8),)),
        "ffn_gain": jnp.clip(1.0 + 0.15 * jax.random.normal(key_list[8], (D,), jnp.float32), 0.25, 1.75),
        "router_weight": normal_values(key_list[9], (D, EXPERTS), (4 * D) ** -0.5, 0.0625, ((0, 8),)),
        "gate_up_weight": normal_values(key_list[10], (EXPERTS, D, 2 * FF), D ** -0.5, 0.125, ((0, 4), (1, 8))),
        "down_weight": normal_values(key_list[11], (EXPERTS, FF, D), (FF // 16) ** -0.5, 0.75, ((0, 4), (1, 8))),
        "cotangent": normal_values(key_list[12], (TOKENS, D), 1.0, 6.0, ((0, 32),)),
    }


EPSILON = 1e-06
ROPE_BASE = 50000.0
PRECISE = lax.Precision.HIGHEST

@jax.custom_vjp
def low(v):
    return lax.optimization_barrier(v.astype(jnp.bfloat16)).astype(jnp.float32)

@jax.custom_vjp
def low_back(v):
    return v

def low_keep(v):
    return (low(v), None)

def low_pass(kept, grad):
    return (grad,)

def back_keep(v):
    return (v, None)

def back_low(kept, grad):
    return (low(grad),)
low.defvjp(low_keep, low_pass)
low_back.defvjp(back_keep, back_low)

def matmul(left, right):
    return jnp.dot(left, right, precision=PRECISE)

def rms_unit(values):
    return values * lax.rsqrt(lax.optimization_barrier(jnp.mean(values * values, -1, keepdims=True)) + EPSILON)

def tables(length, head_size):
    half_size = head_size // 2
    frequency = ROPE_BASE ** (-(jnp.arange(half_size, dtype=jnp.float32) * 2.0 / head_size))
    angles = jnp.arange(length, dtype=jnp.float32)[:, None] * frequency[None, :]
    angles = jnp.concatenate([angles, angles], 1)
    return (jnp.cos(angles)[:, None, :], jnp.sin(angles)[:, None, :])

def rotate(values, cos_table, sine_table):
    half_size = values.shape[-1] // 2
    turned = jnp.concatenate([-values[..., half_size:], values[..., :half_size]], -1)
    return values * cos_table + turned * sine_table

def group_forward(source, expert_ids, slot_ids, params):
    attn_gain, qkv_weight, query_gain, key_gain, out_weight, ffn_gain, router_weight, gate_up_weight, down_weight = params
    group_size = source.shape[0]
    row_count = group_size * TOK_DEV
    score_scale = HD ** (-0.5)
    flat_rows = source.reshape(row_count, D)
    normed = low(rms_unit(flat_rows) * attn_gain)
    projected = low_back(matmul(normed, qkv_weight))
    queries = projected[:, :D].reshape(group_size, TOK_DEV, H, HD)
    keys_raw = projected[:, D:2 * D].reshape(group_size, TOK_DEV, H, HD)
    values_raw = projected[:, 2 * D:].reshape(group_size, TOK_DEV, H, HD)
    cos_table, sine_table = tables(TOK_DEV, HD)
    query_rot = low(rotate(rms_unit(queries) * query_gain, cos_table, sine_table))
    key_rot = low(rotate(rms_unit(keys_raw) * key_gain, cos_table, sine_table))
    value_low = low(values_raw)
    scores = low_back(jnp.einsum('gqhd,gkhd->ghqk', query_rot, key_rot, precision=PRECISE) * score_scale)
    prob_low = low(jax.nn.softmax(scores, -1))
    mixed_heads = jnp.einsum('ghqk,gkhd->gqhd', prob_low, value_low, precision=PRECISE).reshape(row_count, D)
    mixed_heads = low(low_back(mixed_heads))
    residual = flat_rows + low_back(matmul(mixed_heads, out_weight))
    normed_two = low(rms_unit(residual) * ffn_gain)
    logits = low_back(matmul(normed_two, router_weight))
    routes = expert_ids.reshape(row_count, TOPK)
    gate_probs = jax.nn.softmax(jnp.take_along_axis(logits, routes, 1), -1)
    block_ids = (jnp.arange(row_count, dtype=jnp.int32) // TOK_DEV)[:, None]
    slot_index = (routes * (group_size * CAP) + block_ids * CAP + slot_ids.reshape(row_count, TOPK)).reshape(-1)
    copies = jnp.broadcast_to(normed_two[:, None, :], (row_count, TOPK, D)).reshape(row_count * TOPK, D)
    buffer = jnp.zeros((EXPERTS * group_size * CAP, D), normed_two.dtype).at[slot_index].set(copies)
    arrived = low_back(buffer).reshape(EXPERTS, group_size * CAP, D)
    gate_up_val = low_back(jnp.einsum('erd,edf->erf', arrived, gate_up_weight, precision=PRECISE))
    activated = low(jax.nn.silu(gate_up_val[..., :FF]) * gate_up_val[..., FF:])
    expert_out = jnp.einsum('erf,efd->erd', activated, down_weight, precision=PRECISE)
    expert_out = low_back(low(expert_out)).reshape(EXPERTS * group_size * CAP, D)
    picked = expert_out[slot_index].reshape(row_count, TOPK, D)
    moe_sum = lax.optimization_barrier(jnp.sum(gate_probs[:, :, None] * picked, 1))
    return (residual + moe_sum).reshape(group_size, TOK_DEV, D)

def reference(layer_input, expert_ids, slot_ids, attn_gain, qkv_weight, query_gain, key_gain, out_weight, ffn_gain, router_weight, gate_up_weight, down_weight, cotangent):
    blocks = TOKENS // TOK_DEV
    group_size = 1
    for option in range(1, blocks + 1):
        if blocks % option == 0 and option * TOK_DEV <= 1024:
            group_size = option
    groups = blocks // group_size
    params = tuple((tensor.astype(jnp.float32) for tensor in (attn_gain, qkv_weight, query_gain, key_gain, out_weight, ffn_gain, router_weight, gate_up_weight, down_weight)))
    source = layer_input.astype(jnp.float32).reshape(groups, group_size, TOK_DEV, D)
    routes = expert_ids.reshape(groups, group_size, TOK_DEV, TOPK)
    places = slot_ids.reshape(groups, group_size, TOK_DEV, TOPK)

    def forward_all(source_all, param_all):

        def forward_one(bundle):
            return group_forward(bundle[0], bundle[1], bundle[2], param_all)
        return lax.map(jax.checkpoint(forward_one), (source_all, routes, places))
    output, pullback = jax.vjp(forward_all, source, params)
    input_grad, gradients = pullback(cotangent.astype(jnp.float32).reshape(output.shape))
    return (output.reshape(TOKENS, D).astype(jnp.bfloat16), input_grad.reshape(TOKENS, D), gradients[0], gradients[1], gradients[2], gradients[3], gradients[4], gradients[5], gradients[6], gradients[7], gradients[8])
```

```python
import jax
import jax.numpy as jnp
from jax import lax
from jax.sharding import Mesh
from jax.sharding import PartitionSpec as P

EPSILON = 1e-06
ROPE_BASE = 50000.0


def normalize(values):
    factor = lax.rsqrt(jnp.mean(values * values, -1, keepdims=True) + EPSILON)
    return (values * factor, factor)


def norm_back(grad_unit, unit_val, factor):
    return factor * (grad_unit - unit_val * jnp.mean(grad_unit * unit_val, -1, keepdims=True))


def tables(length, head_size):
    half_size = head_size // 2
    frequency = ROPE_BASE ** (-(jnp.arange(half_size, dtype=jnp.float32) * 2.0 / head_size))
    angles = jnp.arange(length, dtype=jnp.float32)[:, None] * frequency[None, :]
    angles = jnp.concatenate([angles, angles], 1)
    return (jnp.cos(angles)[:, None, :], jnp.sin(angles)[:, None, :])


def rotate(values, cos_table, sine_table):
    half_size = values.shape[-1] // 2
    turned = jnp.concatenate([-values[..., half_size:], values[..., :half_size]], -1)
    return values * cos_table + turned * sine_table


def rotate_back(gradient, cos_table, sine_table):
    half_size = gradient.shape[-1] // 2
    turned_grad = gradient * sine_table
    return gradient * cos_table + jnp.concatenate(
        [turned_grad[..., half_size:], -turned_grad[..., :half_size]], -1
    )


def ring_step(value, axis, size, shift=1):
    return lax.ppermute(value, axis, [(i, (i + shift) % size) for i in range(size)])


def gather_slots(value, axis, size):
    slots = [value]
    for _ in range(size - 1):
        value = ring_step(value, axis, size)
        slots.append(value)
    return slots


def add_low(received, own):
    return (received.astype(jnp.float32) + own.astype(jnp.float32)).astype(jnp.bfloat16)


def reduce_slots(parts, axis, size):
    if size == 1:
        return parts[0]
    total = parts[1]
    for s in range(2, size):
        total = add_low(ring_step(total, axis, size), parts[s])
    return add_low(ring_step(total, axis, size), parts[0])


def behind(place, size):
    return (place - jnp.arange(size, dtype=jnp.int32)) % size


def split_rows(value, count):
    rows = value.shape[0] // count
    return [value[i * rows : (i + 1) * rows] for i in range(count)]


def make_local(sizes):
    ny, nc, nz, nx = sizes

    def expert_matrix(shard):
        z_place, x_place = lax.axis_index("z"), lax.axis_index("x")
        rows, columns = shard.shape[1:]
        whole = jnp.zeros((nz, nx, rows, columns), shard.dtype)
        for s in range(nz):
            piece = lax.dynamic_index_in_dim(shard, (z_place + s) % nz, 0, False)
            if s:
                piece = ring_step(piece, "z", nz, s)
            for t, block in enumerate(gather_slots(piece, "x", nx)):
                whole = lax.dynamic_update_slice(
                    whole, block[None, None], ((z_place - s) % nz, (x_place - t) % nx, 0, 0)
                )
        return whole.reshape(nz * nx * rows, columns)

    def expert_gradient(whole):
        z_place, x_place = lax.axis_index("z"), lax.axis_index("x")
        rows, columns = whole.shape[0] // (nz * nx), whole.shape[1]
        whole = whole.reshape(nz, nx, rows, columns)
        result = jnp.zeros((nz, rows, columns), jnp.float32)
        for s in range(nz):
            parts = [
                lax.dynamic_slice(
                    whole,
                    ((z_place + s) % nz, (x_place - t) % nx, 0, 0),
                    (1, 1, rows, columns),
                ).reshape(rows, columns)
                for t in range(nx)
            ]
            piece = reduce_slots(parts, "x", nx)
            if s:
                piece = ring_step(piece, "z", nz, s)
            result = lax.dynamic_update_slice(
                result, piece.astype(jnp.float32)[None], ((z_place - s) % nz, 0, 0)
            )
        return result

    def token_slots(rows):
        chunks = []
        for block in gather_slots(rows, "z", nz):
            joined = jnp.concatenate(gather_slots(block, "y", ny), 0)
            chunks.append(jnp.concatenate(gather_slots(joined, "c", nc), 0))
        return chunks

    def token_sums(chunks):
        parts = []
        for chunk in chunks:
            joined = reduce_slots(split_rows(chunk, nc), "c", nc)
            parts.append(reduce_slots(split_rows(joined, ny), "y", ny))
        return reduce_slots(parts, "z", nz)

    def slot_blocks(rows_by_place):
        out = jnp.take(rows_by_place, behind(lax.axis_index("z"), nz), axis=0)
        out = jnp.take(out, behind(lax.axis_index("c"), nc), axis=1)
        return jnp.take(out, behind(lax.axis_index("y"), ny), axis=2)

    def place_blocks(by_slot):
        return slot_blocks(by_slot)

    def grad_rows(rows, model_width):
        part = model_width // (nz * nx * ny * nc)
        flipped = rows.T.reshape(nz, nx, ny, nc, part, rows.shape[0])
        flipped = jnp.take(flipped, behind(lax.axis_index("z"), nz), axis=0)
        flipped = jnp.take(flipped, behind(lax.axis_index("x"), nx), axis=1)
        flipped = jnp.take(flipped, behind(lax.axis_index("y"), ny), axis=2)
        flipped = jnp.take(flipped, behind(lax.axis_index("c"), nc), axis=3)
        return flipped.transpose(3, 2, 1, 0, 4, 5).reshape(model_width, rows.shape[0])

    def weight_sum(left, right):
        full = jnp.dot(left, right, preferred_element_type=jnp.float32).astype(jnp.bfloat16)
        for axis, size in (("c", nc), ("y", ny), ("x", nx), ("z", nz)):
            full = reduce_slots(split_rows(full, size), axis, size)
        return full

    def local(
        layer_input,
        expert_ids,
        slot_ids,
        attn_gain,
        qkv_weight,
        query_gain,
        key_gain,
        out_weight,
        ffn_gain,
        router_weight,
        gate_up_weight,
        down_weight,
        cotangent,
    ):
        tokens, model_width = layer_input.shape
        head_size = query_gain.shape[0]
        head_count = model_width // head_size
        experts = router_weight.shape[1]
        hidden = gate_up_weight.shape[2] // 2
        score_scale = head_size ** (-0.5)
        replica = lax.axis_index("y") * nc + lax.axis_index("c")
        expert = replica * nz + lax.axis_index("z")

        def own_rows(shard):
            part = shard.shape[0] // (ny * nc)
            return lax.dynamic_slice_in_dim(shard, replica * part, part, 0)

        everywhere = ("z", "x", "y", "c")
        qkv_full = lax.all_gather(own_rows(qkv_weight), everywhere, axis=0, tiled=True)
        out_full = lax.all_gather(own_rows(out_weight), everywhere, axis=0, tiled=True)
        router_full = lax.all_gather(router_weight, ("z", "x"), axis=0, tiled=True)
        all_ids = lax.all_gather(expert_ids, ("z", "c", "y"), axis=0, tiled=True)
        all_ids = slot_blocks(all_ids.reshape((nz, nc, ny) + expert_ids.shape))
        all_ids = all_ids.reshape(nz, nc * ny * tokens, expert_ids.shape[1])
        gate_up_full = expert_matrix(gate_up_weight)
        down_full = expert_matrix(down_weight)
        upstream_rows = token_slots(cotangent)

        source = layer_input.astype(jnp.float32)
        unit_one, factor_one = normalize(source)
        normed = (unit_one * attn_gain).astype(jnp.bfloat16)
        projected = jnp.dot(normed, qkv_full, preferred_element_type=jnp.float32)
        queries = projected[:, :model_width].reshape(tokens, head_count, head_size)
        keys_raw = projected[:, model_width : 2 * model_width].reshape(
            tokens, head_count, head_size
        )
        values_raw = projected[:, 2 * model_width :].reshape(tokens, head_count, head_size)
        unit_query, factor_query = normalize(queries)
        unit_key, factor_key = normalize(keys_raw)
        cos_table, sine_table = tables(tokens, head_size)
        query_rot = rotate(unit_query * query_gain, cos_table, sine_table).astype(jnp.bfloat16)
        key_rot = rotate(unit_key * key_gain, cos_table, sine_table).astype(jnp.bfloat16)
        value_low = values_raw.astype(jnp.bfloat16)
        scores = (
            jnp.einsum("qhd,khd->hqk", query_rot, key_rot, preferred_element_type=jnp.float32)
            * score_scale
        )
        top_score = jnp.max(scores, -1, keepdims=True)
        weights_raw = jnp.exp(scores - top_score)
        totals = jnp.sum(weights_raw, -1, keepdims=True)
        log_total = top_score + jnp.log(totals)
        prob_low = (weights_raw / totals).astype(jnp.bfloat16)
        mixed_heads = jnp.einsum(
            "hqk,khd->qhd", prob_low, value_low, preferred_element_type=jnp.float32
        )
        mixed_low = mixed_heads.reshape(tokens, model_width).astype(jnp.bfloat16)
        residual = source + jnp.dot(mixed_low, out_full, preferred_element_type=jnp.float32)
        unit_two, factor_two = normalize(residual)
        normed_two = (unit_two * ffn_gain).astype(jnp.bfloat16)

        def gates_of(rows, ids):
            logits = jnp.dot(rows, router_full, preferred_element_type=jnp.float32)
            named = jnp.any(
                ids[:, :, None] == jnp.arange(experts, dtype=jnp.int32)[None, None, :], 1
            )
            top = jnp.max(jnp.where(named, logits, -jnp.inf), -1, keepdims=True)
            raw = jnp.where(named, jnp.exp(jnp.where(named, logits - top, 0.0)), 0.0)
            return raw / jnp.sum(raw, -1, keepdims=True)

        rows_in = token_slots(normed_two)
        mine = (jnp.arange(experts, dtype=jnp.int32) == expert).astype(jnp.float32)
        kept = [None] * nz
        dot_parts = [None] * nz
        row_grads = [None] * nz
        for s in [*range(1, nz), 0]:
            rows, upstream_s = rows_in[s], upstream_rows[s]
            gate_mine = jnp.sum(gates_of(rows, all_ids[s]) * mine, -1, keepdims=True)
            both = jnp.dot(rows, gate_up_full, preferred_element_type=jnp.float32)
            gate_part, up_part = both[:, :hidden], both[:, hidden:]
            raw_grad = lax.dot_general(
                upstream_s, down_full, (((1,), (1,)), ((), ())), preferred_element_type=jnp.float32
            )
            sigmoid_gate = jax.nn.sigmoid(gate_part)
            activated = gate_part * sigmoid_gate * up_part
            dot_parts[s] = jnp.sum(activated * raw_grad, -1)
            act_grad = gate_mine * raw_grad
            gate_grad_part = (
                act_grad * up_part * sigmoid_gate * (1.0 + gate_part * (1.0 - sigmoid_gate))
            )
            up_grad_part = act_grad * gate_part * sigmoid_gate
            both_grad = jnp.concatenate([gate_grad_part, up_grad_part], -1).astype(jnp.bfloat16)
            row_grads[s] = lax.dot_general(
                both_grad,
                gate_up_full,
                (((1,), (1,)), ((), ())),
                preferred_element_type=jnp.float32,
            ).astype(jnp.bfloat16)
            kept[s] = (both_grad, (gate_mine * activated).astype(jnp.bfloat16))
        routed_back = token_sums(row_grads)
        by_place = place_blocks(jnp.stack(dot_parts).reshape(nz, nc, ny, tokens))
        gate_dots = lax.all_to_all(
            by_place.transpose(2, 1, 0, 3).reshape(ny * nc * nz, tokens),
            ("y", "c", "z"),
            0,
            0,
            tiled=True,
        ).T

        gated = jnp.concatenate([k[1] for k in kept], 0)
        both_grads = jnp.concatenate([k[0] for k in kept], 0)
        all_rows = jnp.concatenate(rows_in, 0)
        all_upstream = jnp.concatenate(upstream_rows, 0)
        moe_rows = jnp.dot(gated, down_full, preferred_element_type=jnp.float32).astype(jnp.bfloat16)
        moe_sum = token_sums(split_rows(moe_rows, nz))
        mixed_out = (residual + moe_sum.astype(jnp.float32)).astype(jnp.bfloat16)
        contract_rows = (((0,), (0,)), ((), ()))
        gate_up_grad = expert_gradient(
            lax.dot_general(
                all_rows, both_grads, contract_rows, preferred_element_type=jnp.float32
            ).astype(jnp.bfloat16)
        )
        down_grad = expert_gradient(
            lax.dot_general(
                gated, all_upstream, contract_rows, preferred_element_type=jnp.float32
            ).astype(jnp.bfloat16)
        )

        upstream = cotangent.astype(jnp.float32)
        gate_probs = gates_of(normed_two, expert_ids)
        chosen_grad = gate_probs * (
            gate_dots - jnp.sum(gate_probs * gate_dots, -1, keepdims=True)
        )
        logit_grad = chosen_grad.astype(jnp.bfloat16)
        router_part = jnp.dot(normed_two.T, logit_grad, preferred_element_type=jnp.float32)
        normed_two_grad = routed_back.astype(jnp.float32) + jnp.dot(
            logit_grad, router_full.T, preferred_element_type=jnp.float32
        )
        ffn_gain_part = jnp.sum(normed_two_grad * unit_two, 0)
        residual_grad = upstream + norm_back(normed_two_grad * ffn_gain, unit_two, factor_two)
        attn_grad_low = residual_grad.astype(jnp.bfloat16)
        mixed_grad = jnp.dot(
            attn_grad_low, out_full.T, preferred_element_type=jnp.float32
        ).astype(jnp.bfloat16)
        out_shard = weight_sum(grad_rows(mixed_low, model_width), attn_grad_low)
        mixed_grad = mixed_grad.reshape(tokens, head_count, head_size)
        value_grad = jnp.einsum(
            "hqk,qhd->khd", prob_low, mixed_grad, preferred_element_type=jnp.float32
        )
        value_grad = value_grad.reshape(tokens, model_width).astype(jnp.bfloat16)
        normed_rows = grad_rows(normed, model_width)
        value_shard = weight_sum(normed_rows, value_grad)
        prob_grad = jnp.einsum(
            "qhd,khd->hqk", mixed_grad, value_low, preferred_element_type=jnp.float32
        )
        scores_again = (
            jnp.einsum("qhd,khd->hqk", query_rot, key_rot, preferred_element_type=jnp.float32)
            * score_scale
        )
        prob_full = jnp.exp(scores_again - log_total)
        score_grad = (
            prob_full * (prob_grad - jnp.sum(prob_full * prob_grad, -1, keepdims=True))
        ).astype(jnp.bfloat16)
        query_grad = (
            jnp.einsum("hqk,khd->qhd", score_grad, key_rot, preferred_element_type=jnp.float32)
            * score_scale
        )
        key_grad = (
            jnp.einsum("hqk,qhd->khd", score_grad, query_rot, preferred_element_type=jnp.float32)
            * score_scale
        )
        query_grad = rotate_back(query_grad, cos_table, sine_table)
        key_grad = rotate_back(key_grad, cos_table, sine_table)
        query_gain_part = jnp.sum(query_grad * unit_query, (0, 1))
        key_gain_part = jnp.sum(key_grad * unit_key, (0, 1))
        query_pre = norm_back(query_grad * query_gain, unit_query, factor_query)
        key_pre = norm_back(key_grad * key_gain, unit_key, factor_key)
        query_pre = query_pre.reshape(tokens, model_width).astype(jnp.bfloat16)
        key_pre = key_pre.reshape(tokens, model_width).astype(jnp.bfloat16)
        query_shard = weight_sum(normed_rows, query_pre)
        key_shard = weight_sum(normed_rows, key_pre)
        qkv_grad_low = jnp.concatenate([query_pre, key_pre, value_grad], 1)
        normed_grad = jnp.dot(qkv_grad_low, qkv_full.T, preferred_element_type=jnp.float32)
        attn_gain_part = jnp.sum(normed_grad * unit_one, 0)
        input_grad = residual_grad + norm_back(normed_grad * attn_gain, unit_one, factor_one)

        def spread(shard):
            return lax.all_gather(shard, ("y", "c"), axis=0, tiled=True).astype(jnp.float32)

        qkv_weight_grad = spread(jnp.concatenate([query_shard, key_shard, value_shard], 1))
        out_weight_grad = spread(out_shard)
        router_sum, attn_gain_grad, query_gain_grad, key_gain_grad, ffn_gain_grad = lax.psum(
            (router_part, attn_gain_part, query_gain_part, key_gain_part, ffn_gain_part),
            ("y", "c", "z", "x"),
        )
        router_rows = router_weight.shape[0]
        router_weight_grad = lax.dynamic_slice_in_dim(
            router_sum,
            (lax.axis_index("z") * nx + lax.axis_index("x")) * router_rows,
            router_rows,
            0,
        )
        return (
            mixed_out,
            input_grad,
            attn_gain_grad,
            qkv_weight_grad,
            query_gain_grad,
            key_gain_grad,
            out_weight_grad,
            ffn_gain_grad,
            router_weight_grad,
            gate_up_grad,
            down_grad,
        )

    return local


def solution(mesh):
    groups, shards = mesh.shape["expert"], mesh.shape["fsdp"]

    def step(*arrays):
        each = arrays[10].shape[0] // groups
        sizes = (groups // 2, 2, each, shards // each)
        cube = Mesh(mesh.devices.reshape(sizes), ("y", "c", "z", "x"))
        group, shard = ("y", "c"), ("z", "x")
        everyone = group + shard
        rows, split = P(everyone, None), P(shard, None)
        experts = P(group, shard, None)
        return jax.shard_map(
            make_local(sizes),
            mesh=cube,
            in_specs=(
                rows,
                rows,
                rows,
                P(),
                split,
                P(),
                P(),
                split,
                P(),
                split,
                experts,
                experts,
                rows,
            ),
            out_specs=(rows, rows, P(), split, P(), P(), split, P(), split, experts, experts),
            check_vma=False,
        )(*arrays)

    return step
```
